32 devices in a mesh: outer: 8 (over z, core), expert: 4 (over y, x).
Axes of the slice: x: 2, y: 2, z: 4, core: 2. Of those that a mesh axis runs over, the one named last changes fastest.
Arguments:
- tokens: bfloat16 [2, 4096, 2048], P(None, ('outer', 'expert')), may hold values from -6 to 6
- cotangent: bfloat16 [2, 4096, 2048], P(None, ('outer', 'expert')), may hold values from -0.59765625 to 0.59765625
- combine: float32 [2, 4096, 2], P(None, ('outer', 'expert')), may hold values from 0.2 to 1
- routing: int32 [2, 4096, 2], P(None, ('outer', 'expert')), may hold values from 0 to 3, all different within a row; in each aligned block of 128 rows (0 to 127, 128 to 255, ..., all dimensions but the last counted through in order) at most 128 rows name the same one
- gate_proj: bfloat16 [4, 2048, 384], P('expert'), may hold values from -0.125 to 0.125
- up_proj: bfloat16 [4, 2048, 384], P('expert'), may hold values from -0.125 to 0.125
- momentum: float32 [8, 4, 384, 2048], P('outer', 'expert'), may hold values from -6 to 6
- freq_rows: int32 [4, 3, 16, 16], P('expert'), may hold values from 0 to 127, all different within a row
Outputs:
- new_momentum: float32 [8, 4, 384, 2048], P('outer', 'expert')
- update: bfloat16 [4, 384, 2048], P('expert')
The draws below stay inside these ranges and needn't reach their ends.
Inputs may be any that keep to these rules, and one draw needn't show every extreme that they name: `routing`: each token names 2 different experts; within one pass, no expert is named by more than 128 of the 128 tokens of one device, and in some devices' blocks an expert is named by exactly 128. `freq_rows`: the 16 rows named for one tile are different.
All inputs are finite; a program needn't handle non-finite values.
Results may differ from the reference program's by a relative error of at most 0.0056.
Values may be sent and summed in bfloat16 or wider, within the bound.
No kernel may reach another device: no remote copies, remote signals or barrier semaphores. Data moves between devices by JAX's collectives and lax.ppermute only.
A program may use at most 128 MiB of HBM per device.

```python
import math
import jax
import jax.numpy as jnp
import numpy as np
from jax import lax

D = 2048
FFW = 384
TILE = 128
K = 16
TOP = 2
PASSES = 2
TOK_DEV = 128
CAP = 128
EXPERTS = 4
TOKENS = 4096
N_OUTER = 8
N_EXPERT = 4


def steps_of(key, shape, shards, low, largest):
    level, own = 1.0, jax.random.fold_in(key, 6)
    for position, shards_of in shards:
        steps = jnp.exp(jax.random.uniform(jax.random.fold_in(own, position), (shards_of,), jnp.float32, low / len(shards), largest / len(shards)))
        level = level * jnp.repeat(steps, shape[position] // shards_of).reshape([-1 if axis == position else 1 for axis in range(len(shape))])
    return level


def distinct(key, rows, number_of, top, lift):
    order = jax.random.permutation(jax.random.fold_in(key, 1), number_of)
    favour = order
    for power in range(3):
        favour = favour * favour // number_of
    favour = favour * lift // number_of
    lots = jax.random.randint(jax.random.fold_in(key, 2), (rows, number_of), 0, 4096) + favour
    holders = jax.random.permutation(jax.random.fold_in(key, 3), rows)[jnp.arange(number_of) % rows]
    lots = jnp.where(jnp.arange(rows)[:, None] == holders[None, :], 1 << 14, lots)
    merit = lots * number_of + jnp.arange(number_of)
    return lax.top_k(merit.astype(jnp.int32), top)[1].astype(jnp.int32)


def shared_out(own_key, own, number, rows, number_of, top, bound, skew):
    sequence = jax.random.permutation(own_key, number_of)
    heavy_load, usual = load_shares(number_of, rows * top, bound, skew, True), load_shares(number_of, rows * top, bound, skew, False)
    places = jnp.arange(number_of)

    def named(sizes, offset_by):
        used = int((sizes > 0).sum())
        fixed = max(1, used // 4)
        shifted = fixed + (places - fixed + offset_by * (used - fixed)) % max(1, number_of - fixed)
        return jnp.zeros((number_of,), jnp.int32).at[sequence[jnp.where(places < fixed, places, shifted)]].set(jnp.asarray(sizes, jnp.int32))

    sizes = jnp.where(number % 4 == 0, named(heavy_load, number // 4), named(usual, number - number // 4 - 1))
    mixed = jax.random.permutation(jax.random.fold_in(own, 3), number_of)
    giver, taker = mixed[0:number_of // 2 * 2:2], mixed[1:number_of // 2 * 2:2]
    room = jnp.minimum(sizes[giver] - 1, bound - sizes[taker]) // 2
    room = jnp.where((giver == sequence[0]) | (taker == sequence[0]) | (sizes[taker] == 0), 0, jnp.maximum(room, 0))
    shifted = jax.random.randint(jax.random.fold_in(own, 4), (number_of // 2,), 0, 1 << 20) % (room + 1)
    sizes = sizes.at[giver].add(-shifted).at[taker].add(shifted)
    labels = jnp.searchsorted(jnp.cumsum(sizes), jnp.arange(rows * top), side="right").astype(jnp.int32)
    table = labels.reshape(top, rows).T
    table = table[jax.random.permutation(jax.random.fold_in(own, 1), rows)]
    offset_by = jax.random.randint(jax.random.fold_in(own, 2), (rows, 1), 0, top)
    return jnp.take_along_axis(table, (jnp.arange(top)[None, :] + offset_by) % top, axis=1)


def load_shares(number_of, total, limit, slope, full):
    weights = [(1 << 20) // math.isqrt(standing ** slope) + 1 for standing in range(1, number_of + 1)]
    largest = limit if full else min(limit, max(-(-total // number_of), total * weights[0] // sum(weights)))
    least = 1 if total - largest >= number_of - 1 else 0
    given, rest = [largest] + [least] * (number_of - 1), total - largest - least * (number_of - 1)
    while rest > 0:
        movable = [i for i in range(1, number_of) if given[i] < largest] or [i for i in range(1, number_of) if given[i] < limit]
        whole, left = sum([weights[i] for i in movable]), rest
        for i in movable:
            addition = min(limit - given[i], max(1, left * weights[i] // whole), rest)
            given[i] = given[i] + addition
            rest = rest - addition
    return np.array(given)


def normal_values(key, extent, width, limit, cuts=(), kind=jnp.bfloat16):
    gain = steps_of(key, extent, cuts, -0.22, 0.18) if cuts else 1.0
    drawn = jax.random.normal(key, extent, jnp.float32) * width * gain
    return jnp.minimum(jnp.maximum(drawn, -limit), limit).astype(kind)


def setup_inputs(seed: int = 0) -> dict:
    keys = jax.random.split(jax.random.key(seed), 9)
    tokens = normal_values(keys[0], (PASSES, TOKENS, D), 1.0, 6.0, ((1, 32),))
    cotangent = normal_values(keys[1], (PASSES, TOKENS, D), 0.1, 0.59765625, ((1, 32),))
    combine = jnp.clip(0.2 + 0.8 * jax.random.uniform(keys[2], (PASSES, TOKENS, TOP), jnp.float32) ** steps_of(keys[2], (PASSES, TOKENS, TOP), ((1, 32),), -0.2, 0.2), 0.2, 1.0)
    routing_keys = jax.random.split(jax.random.fold_in(keys[3], 1), PASSES * TOKENS // TOK_DEV)
    routing_turns = jax.random.permutation(jax.random.fold_in(keys[3], 3), PASSES * TOKENS // TOK_DEV)
    routing = jax.vmap(lambda own, number: shared_out(jax.random.fold_in(keys[3], 2), own, number, TOK_DEV, N_EXPERT, TOP, CAP, 1))(routing_keys, routing_turns).reshape((PASSES, TOKENS, TOP))
    gate_proj = normal_values(keys[4], (EXPERTS, D, FFW), D ** -0.5, 0.125, ((0, 4),))
    up_proj = normal_values(keys[5], (EXPERTS, D, FFW), D ** -0.5, 0.125, ((0, 4),))
    momentum = normal_values(keys[6], (N_OUTER, EXPERTS, FFW, D), 1.0, 6.0, ((0, 8), (1, 4)), jnp.float32)
    freq_rows = distinct(keys[7], EXPERTS * (FFW // TILE) * (D // TILE), TILE, K, 0).reshape((EXPERTS, FFW // TILE, D // TILE, K))
    return {"tokens": tokens, "cotangent": cotangent, "combine": combine, "routing": routing, "gate_proj": gate_proj, "up_proj": up_proj, "momentum": momentum, "freq_rows": freq_rows}


decay_rate = 0.9

def cosine_table():
    freq = jnp.arange(TILE, dtype=jnp.float32)[:, None]
    place = jnp.arange(TILE, dtype=jnp.float32)[None, :]
    scale = jnp.where(freq == 0, jnp.sqrt(1.0 / TILE), jnp.sqrt(2.0 / TILE))
    return scale * jnp.cos(jnp.pi * (2.0 * place + 1.0) * freq / (2.0 * TILE))

def to_freq(matrix, table):
    blocks = matrix.reshape(FFW // TILE, TILE, D // TILE, TILE)
    return jnp.einsum('ij,ajbk,lk->aibl', table, blocks, table, precision=lax.Precision.HIGHEST)

def from_freq(spectrum, table):
    blocks = jnp.einsum('ij,aibl,lk->ajbk', table, spectrum, table, precision=lax.Precision.HIGHEST)
    return blocks.reshape(FFW, D)

def scatter_rows(token_block, grad_block, weight_block, route_block):
    flat_routes = route_block.reshape(-1)
    onehot = (flat_routes[:, None] == jnp.arange(N_EXPERT, dtype=jnp.int32)[None, :]).astype(jnp.int32)
    slot_of = lax.optimization_barrier(jnp.sum((jnp.cumsum(onehot, axis=0) - 1) * onehot, axis=1))
    target = (flat_routes * CAP + slot_of).astype(jnp.int32)
    features = jnp.repeat(token_block, TOP, axis=0)
    scaled = (weight_block.reshape(-1)[:, None] * jnp.repeat(grad_block, TOP, axis=0).astype(jnp.float32)).astype(jnp.bfloat16)
    buffer_x = jnp.zeros((N_EXPERT * CAP, D), jnp.bfloat16).at[target].set(features)
    buffer_g = jnp.zeros((N_EXPERT * CAP, D), jnp.bfloat16).at[target].set(scaled)
    return (buffer_x.reshape(N_EXPERT, CAP, D), buffer_g.reshape(N_EXPERT, CAP, D))

def expert_grad(pieces):
    rows_x, rows_g, gate_weight, up_weight = pieces
    gate = jnp.dot(rows_x, gate_weight, preferred_element_type=jnp.float32)
    upper = jnp.dot(rows_x, up_weight, preferred_element_type=jnp.float32)
    hidden = (jax.nn.silu(gate) * upper).astype(jnp.bfloat16)
    return lax.dot_general(hidden, rows_g, (((0,), (0,)), ((), ())), preferred_element_type=jnp.float32)

def reference(tokens, cotangent, combine, routing, gate_proj, up_proj, momentum, freq_rows):
    table = cosine_table()
    picker = (freq_rows[..., None] == jnp.arange(TILE, dtype=jnp.int32)).astype(jnp.float32)

    def regroup(array):
        shaped = array.reshape((PASSES, N_OUTER, N_EXPERT, TOK_DEV) + array.shape[2:])
        return jnp.moveaxis(shaped, 1, 0)

    def replica(inputs):
        token_part, grad_part, weight_part, route_part, moment_in = inputs
        buffer_x, buffer_g = jax.vmap(jax.vmap(scatter_rows))(token_part, grad_part, weight_part, route_part)
        buffer_x = jnp.moveaxis(buffer_x, 2, 0).reshape(N_EXPERT, -1, D)
        buffer_g = jnp.moveaxis(buffer_g, 2, 0).reshape(N_EXPERT, -1, D)
        gradient = lax.map(expert_grad, (buffer_x, buffer_g, gate_proj, up_proj))
        moment = decay_rate * moment_in + gradient
        spectrum = jax.vmap(lambda matrix: to_freq(matrix, table))(moment)
        sent = jnp.einsum('eabki,eaibl->eabkl', picker, spectrum, precision=lax.Precision.HIGHEST)
        placed = jnp.einsum('eabki,eabkl->eaibl', picker, sent, precision=lax.Precision.HIGHEST)
        removed = jax.vmap(lambda spec: from_freq(spec, table))(placed)
        return (moment - removed, sent)
    new_momentum, sent_all = lax.map(replica, (regroup(tokens), regroup(cotangent), regroup(combine), regroup(routing), momentum))
    averaged = lax.optimization_barrier(jnp.sum(sent_all, axis=0)) / N_OUTER
    placed = jnp.einsum('eabki,eabkl->eaibl', picker, averaged, precision=lax.Precision.HIGHEST)
    update = jax.vmap(lambda spec: from_freq(spec, table))(placed).astype(jnp.bfloat16)
    return (new_momentum, update)
```

```python
import functools
import jax
import jax.numpy as jnp
import numpy as np
from jax import lax
from jax.experimental import pallas as pl
from jax.experimental.pallas import tpu as pltpu
from jax.sharding import PartitionSpec as P

TILE = 128
DECAY = 0.9
CHUNKS = (768, 768, 512)
COLS = 256


def cosine_parts():
    freq = np.arange(TILE, dtype=np.float64)[:, None]
    place = np.arange(TILE, dtype=np.float64)[None, :]
    scale = np.where(freq == 0, np.sqrt(1.0 / TILE), np.sqrt(2.0 / TILE))
    table = scale * np.cos(np.pi * (2.0 * place + 1.0) * freq / (2.0 * TILE))
    high = table.astype(jnp.bfloat16)
    low = (table - high.astype(np.float64)).astype(jnp.bfloat16)
    return np.concatenate([high, low], axis=1)


def rows_kernel(tiles, keep, pick_ref, table_ref, sel_ref, selt_ref):
    for t in range(tiles):
        both = jnp.dot(pick_ref[t], table_ref[...], preferred_element_type=jnp.float32)
        high, low = both[:, :TILE], both[:, TILE:]
        sel_ref[t] = jnp.concatenate([high, low], axis=0).astype(jnp.bfloat16)
        pad = jnp.zeros((TILE - 3 * keep, TILE), jnp.float32)
        stack = jnp.concatenate([high, low, high, pad], axis=0)
        selt_ref[t] = stack.T[:, : 3 * keep].astype(jnp.bfloat16)


def chosen_rows(freq_rows, table):
    a, b, keep = freq_rows.shape
    pick = (freq_rows[..., None] == jnp.arange(TILE, dtype=jnp.int32)).astype(jnp.bfloat16)
    pick = pick.reshape(a * b, keep, TILE)
    step = 8
    spec = lambda r, c: pl.BlockSpec((step, r, c), lambda i: (i, 0, 0))
    sel, selt = pl.pallas_call(
        functools.partial(rows_kernel, step, keep),
        grid=(a * b // step,),
        in_specs=[spec(keep, TILE), pl.BlockSpec(table.shape, lambda i: (0, 0))],
        out_specs=[spec(2 * keep, TILE), spec(TILE, 3 * keep)],
        out_shape=[
            jax.ShapeDtypeStruct((a * b, 2 * keep, TILE), jnp.bfloat16),
            jax.ShapeDtypeStruct((a * b, TILE, 3 * keep), jnp.bfloat16),
        ],
        cost_estimate=pl.CostEstimate(flops=50_000_000, bytes_accessed=4_000_000, transcendentals=0),
        name="chosen_rows",
    )(pick, table)
    return sel.reshape(a, b, 2 * keep, TILE), selt.reshape(a, b, TILE, 3 * keep)


def hidden_kernel(count, weight_ref, *refs):
    x_refs, (gate_ref, up_ref, out_ref, gate_acc, up_acc) = refs[:count], refs[count:]
    step = pl.program_id(0)

    @pl.when(step == 0)
    def _():
        gate_acc[...] = jnp.zeros_like(gate_acc)
        up_acc[...] = jnp.zeros_like(up_acc)

    gate_w, up_w = gate_ref[...], up_ref[...]
    row = 0
    for x_ref in x_refs:
        x = x_ref[...].reshape(-1, x_ref.shape[-1])
        here = pl.ds(row, x.shape[0])
        gate_acc[here, :] += jnp.dot(x, gate_w, preferred_element_type=jnp.float32)
        up_acc[here, :] += jnp.dot(x, up_w, preferred_element_type=jnp.float32)
        row += x.shape[0]

    @pl.when(step == pl.num_programs(0) - 1)
    def _():
        size = weight_ref.shape[1]
        eye = lax.broadcasted_iota(jnp.int32, (size, size), 0) == lax.broadcasted_iota(
            jnp.int32, (size, size), 1
        )
        for i in range(weight_ref.shape[0]):
            here = pl.ds(i * size, size)
            gate, up = gate_acc[here, :], up_acc[here, :]
            weight = jnp.sum(jnp.where(eye, weight_ref[pl.ds(i, 1), :], 0.0), axis=1, keepdims=True)
            hidden = gate / (1.0 + jnp.exp(-gate)) * up * weight
            out_ref[:, here] = hidden.T.astype(jnp.bfloat16)


def hidden_rows(blocks, weights, gate_w, up_w):
    depth, units = gate_w.shape
    rows = weights.shape[0] * weights.shape[1]
    step = depth // 4
    x_specs = [
        pl.BlockSpec(x.shape[:-1] + (step,), lambda k, n=x.ndim: (0,) * (n - 1) + (k,)) for x in blocks
    ]
    w_spec = pl.BlockSpec((step, units), lambda k: (k, 0))
    return pl.pallas_call(
        functools.partial(hidden_kernel, len(blocks)),
        grid=(depth // step,),
        in_specs=[pl.BlockSpec(weights.shape, lambda k: (0, 0))] + x_specs + [w_spec, w_spec],
        out_specs=pl.BlockSpec((units, rows), lambda k: (0, 0)),
        out_shape=jax.ShapeDtypeStruct((units, rows), jnp.bfloat16),
        scratch_shapes=[pltpu.VMEM((rows, units), jnp.float32)] * 2,
        cost_estimate=pl.CostEstimate(
            flops=4 * rows * depth * units,
            bytes_accessed=2 * (rows * depth + 2 * depth * units + rows * units),
            transcendentals=rows * units,
        ),
        name="hidden_rows",
    )(weights, *blocks, gate_w, up_w)


def split(value):
    high = value.astype(jnp.bfloat16)
    return high, (value - high.astype(jnp.float32)).astype(jnp.bfloat16)


def moment_kernel(h_count, g_count, keep, *refs):
    h_refs, g_refs = refs[:h_count], refs[h_count : h_count + g_count]
    mom_ref, sel_ref, selt_ref = refs[h_count + g_count : h_count + g_count + 3]
    new_ref, sent_ref = refs[-2:]
    hidden = jnp.concatenate([r[...] for r in h_refs], axis=1)
    grads = jnp.concatenate([r[...].reshape(-1, r.shape[-1]) for r in g_refs], axis=0)
    moment = DECAY * mom_ref[...] + jnp.dot(hidden, grads, preferred_element_type=jnp.float32)
    for a in range(sel_ref.shape[0]):
        for b in range(sel_ref.shape[1]):
            block = moment[a * TILE : (a + 1) * TILE, b * TILE : (b + 1) * TILE]
            high, low = split(block)
            first = jnp.dot(sel_ref[a, b], high, preferred_element_type=jnp.float32)
            second = jnp.dot(sel_ref[a, b, :keep], low, preferred_element_type=jnp.float32)
            sent = first[:keep] + first[keep:] + second
            sent_high, sent_low = split(sent)
            sent_ref[a, b] = sent_high
            stack = jnp.concatenate([sent_high, sent_high, sent_low], axis=0)
            removed = jnp.dot(selt_ref[a, b], stack, preferred_element_type=jnp.float32)
            new_ref[a * TILE : (a + 1) * TILE, b * TILE : (b + 1) * TILE] = block - removed


def moment_columns(start, hiddens, own, grads, momentum, sel, selt, buffer):
    units, width = momentum.shape
    size = grads[0].shape[-1]
    keep = sel.shape[2] // 2
    wide = sel.shape[0]
    first, tiles = start // COLS, COLS // TILE
    at = lambda lead, off: lambda j: (0,) * lead + (j + off,)
    h_specs = [pl.BlockSpec(h.shape, lambda j: (0, 0)) for h in hiddens]
    g_specs = [pl.BlockSpec(own.shape[:-1] + (COLS,), at(2, first))]
    g_specs += [pl.BlockSpec(g.shape[:-1] + (COLS,), at(g.ndim - 1, 0)) for g in grads]
    rest = [
        pl.BlockSpec((units, COLS), at(1, first)),
        pl.BlockSpec((wide, tiles) + sel.shape[2:], lambda j: (0, j + first, 0, 0)),
        pl.BlockSpec((wide, tiles) + selt.shape[2:], lambda j: (0, j + first, 0, 0)),
    ]
    args = [*hiddens, own, *grads, momentum, sel, selt]
    alias = {}
    if buffer is not None:
        rest.append(pl.BlockSpec(memory_space=pl.ANY))
        alias = {len(args): 0}
        args.append(buffer)
    rows = sum(h.shape[1] for h in hiddens)
    return pl.pallas_call(
        functools.partial(moment_kernel, len(hiddens), 1 + len(grads), keep),
        grid=(size // COLS,),
        in_specs=h_specs + g_specs + rest,
        out_specs=[
            pl.BlockSpec((units, COLS), at(1, first)),
            pl.BlockSpec((wide, tiles, keep, TILE), lambda j: (0, j, 0, 0)),
        ],
        out_shape=[
            jax.ShapeDtypeStruct((units, width), jnp.float32),
            jax.ShapeDtypeStruct((wide, size // TILE, keep, TILE), jnp.bfloat16),
        ],
        input_output_aliases=alias,
        cost_estimate=pl.CostEstimate(
            flops=2 * rows * units * size,
            bytes_accessed=size * (8 * units + 2 * rows) + 2 * units * rows,
            transcendentals=0,
        ),
        name="moment_columns",
    )(*args)


def update_kernel(scale, mine_ref, theirs_ref, selt_ref, *refs):
    out_ref = refs[-1]
    for a in range(selt_ref.shape[0]):
        for b in range(selt_ref.shape[1]):
            total = mine_ref[a, b].astype(jnp.float32) + theirs_ref[a, b].astype(jnp.float32)
            high, low = split(total * scale)
            stack = jnp.concatenate([high, high, low], axis=0)
            block = jnp.dot(selt_ref[a, b], stack, preferred_element_type=jnp.float32)
            out_ref[a * TILE : (a + 1) * TILE, b * TILE : (b + 1) * TILE] = block.astype(jnp.bfloat16)


def update_columns(start, mine, theirs, selt, scale, shape, buffer):
    wide, tiles = mine.shape[:2]
    per = COLS // TILE
    first = start // COLS
    sums = pl.BlockSpec((wide, per) + mine.shape[2:], lambda j: (0, j, 0, 0))
    specs = [sums, sums, pl.BlockSpec((wide, per) + selt.shape[2:], lambda j: (0, j + first, 0, 0))]
    args, alias = [mine, theirs, selt], {}
    if buffer is not None:
        specs.append(pl.BlockSpec(memory_space=pl.ANY))
        alias = {len(args): 0}
        args.append(buffer)
    return pl.pallas_call(
        functools.partial(update_kernel, scale),
        grid=(tiles // per,),
        in_specs=specs,
        out_specs=pl.BlockSpec((shape[0], COLS), lambda j: (0, j + first)),
        out_shape=jax.ShapeDtypeStruct(shape, jnp.bfloat16),
        input_output_aliases=alias,
        cost_estimate=pl.CostEstimate(
            flops=2 * 48 * shape[0] * tiles * TILE, bytes_accessed=3 * shape[0] * tiles * TILE, transcendentals=0
        ),
        name="update_columns",
    )(*args)


def on_device(tokens, cotangent, combine, routing, gate_proj, up_proj, momentum, freq_rows):
    experts, replicas = lax.axis_size("expert"), lax.axis_size("outer")
    me = lax.axis_index("expert")
    gate_w, up_w, moment = gate_proj[0], up_proj[0], momentum[0, 0]
    passes, count, width = tokens.shape

    def swap(array, mask):
        return lax.ppermute(array, "expert", [(e, e ^ mask) for e in range(experts)])

    others = range(1, experts)
    named = routing[:, None, :, :] == jnp.arange(experts, dtype=jnp.int32)[None, :, None, None]
    weight = jnp.sum(jnp.where(named, combine[:, None, :, :], 0.0), axis=3)
    weight_for = lambda e: lax.dynamic_index_in_dim(weight, e, axis=1, keepdims=False)
    square = experts == 4

    def gather(first, second):
        if square:
            x0, y1 = swap(first, 1), swap(second, 2)
            x1, y0 = swap(second, 1), swap(first, 2)
            return {1: [x0, x1], 2: [y0, y1], 3: [swap(x0, 2), swap(y1, 1)]}
        return {m: [swap(first, m), swap(second, m)] for m in others}

    def gather_pair(pair):
        if square:
            x, y = swap(pair, 1), swap(pair, 2)
            return {1: [x], 2: [y], 3: [swap(x[0], 2), swap(y[1], 1)]}
        return {m: [swap(pair, m)] for m in others}

    blocks = gather(tokens[0], tokens[1])
    weights = {m: swap(weight_for(me ^ m), m) for m in others}
    table = jnp.asarray(cosine_parts())
    sel, selt = chosen_rows(freq_rows[0], table)
    hiddens = [hidden_rows([tokens], weight_for(me), gate_w, up_w)]
    groups = [(1, 2), (3,)] if square else [(m,) for m in others]
    for group in groups:
        parts = sum([blocks[m] for m in group], [])
        scale = jnp.concatenate([weights[m] for m in group], axis=0)
        hiddens.append(hidden_rows(parts, scale, gate_w, up_w))

    start, buffer, out = 0, None, None
    for size in CHUNKS:
        pieces = gather_pair(cotangent[:, :, start : start + size])
        grads = sum([pieces[m] for m in others], [])
        buffer, sent = moment_columns(start, hiddens, cotangent, grads, moment, sel, selt, buffer)
        mask = 1
        while True:
            theirs = lax.ppermute(sent, "outer", [(o, o ^ mask) for o in range(replicas)])
            mask *= 2
            if mask >= replicas:
                break
            sent = (sent.astype(jnp.float32) + theirs.astype(jnp.float32)).astype(jnp.bfloat16)
        out = update_columns(start, sent, theirs, selt, 1.0 / replicas, moment.shape, out)
        start += size
    return buffer[None, None], out[None]


def solution(mesh):
    placed = (
        P(None, ("outer", "expert"), None),
        P(None, ("outer", "expert"), None),
        P(None, ("outer", "expert"), None),
        P(None, ("outer", "expert"), None),
        P("expert", None, None),
        P("expert", None, None),
        P("outer", "expert", None, None),
        P("expert", None, None, None),
    )
    return jax.shard_map(
        on_device,
        mesh=mesh,
        in_specs=placed,
        out_specs=(P("outer", "expert", None, None), P("expert", None, None)),
        check_vma=False,
    )
```

```python
import functools
import jax
import jax.numpy as jnp
import numpy as np
from jax import lax
from jax.experimental import pallas as pl
from jax.experimental.pallas import tpu as pltpu
from jax.sharding import PartitionSpec as P


TILE = 128
DECAY = 0.9
CHUNKS = (768, 768, 512)
COLS = 256
WHOLE = pl.BlockSpec(memory_space=pltpu.VMEM)
PARAMS = pltpu.CompilerParams(vmem_limit_bytes=12 << 20)


def cosine_parts():
    freq = np.arange(TILE, dtype=np.float64)[:, None]
    place = np.arange(TILE, dtype=np.float64)[None, :]
    scale = np.where(freq == 0, np.sqrt(1.0 / TILE), np.sqrt(2.0 / TILE))
    table = scale * np.cos(np.pi * (2.0 * place + 1.0) * freq / (2.0 * TILE))
    high = table.astype(jnp.bfloat16)
    low = (table - high.astype(np.float64)).astype(jnp.bfloat16)
    return np.concatenate([high, low], axis=1)


def split(value):
    high = value.astype(jnp.bfloat16)
    return high, (value - high.astype(jnp.float32)).astype(jnp.bfloat16)


def rows_kernel(keep, pick_ref, table_ref, sel_ref, selt_ref):
    pad = jnp.zeros((TILE - 3 * keep, TILE), jnp.float32)

    @pl.loop(0, pick_ref.shape[0] // 8)
    def _(group):
        for t in range(8):
            tile = group * 8 + t
            both = jnp.dot(pick_ref[tile], table_ref[...], preferred_element_type=jnp.float32)
            high, low = both[:, :TILE], both[:, TILE:]
            sel_ref[tile] = jnp.concatenate([high, low], axis=0).astype(jnp.bfloat16)
            stack = jnp.concatenate([high, low, high, pad], axis=0)
            selt_ref[tile] = stack.T[:, : 3 * keep].astype(jnp.bfloat16)


def chosen_rows(freq_rows, table):
    a, b, keep = freq_rows.shape
    pick = (freq_rows[..., None] == jnp.arange(TILE, dtype=jnp.int32)).astype(jnp.bfloat16)
    pick = pick.reshape(a * b, keep, TILE)
    sel, selt = pl.pallas_call(
        functools.partial(rows_kernel, keep),
        in_specs=[WHOLE] * 2,
        out_specs=[WHOLE] * 2,
        out_shape=[
            jax.ShapeDtypeStruct((a * b, 2 * keep, TILE), jnp.bfloat16),
            jax.ShapeDtypeStruct((a * b, TILE, 3 * keep), jnp.bfloat16),
        ],
        compiler_params=PARAMS,
        cost_estimate=pl.CostEstimate(flops=50_000_000, bytes_accessed=4_000_000, transcendentals=0),
        name="chosen_rows",
    )(pick, table)
    return sel.reshape(a, b, 2 * keep, TILE), selt.reshape(a, b, TILE, 3 * keep)


def hidden_kernel(places, count, *refs):
    w_refs, x_refs = refs[:count], refs[count:-3]
    gate_ref, up_ref, out_ref = refs[-3:]
    size = x_refs[0].shape[-2]
    eye = lax.broadcasted_iota(jnp.int32, (size, size), 0) == lax.broadcasted_iota(
        jnp.int32, (size, size), 1
    )
    x = jnp.concatenate([r[...].reshape(-1, r.shape[-1]) for r in x_refs], axis=0)
    gate = jnp.dot(x, gate_ref[...], preferred_element_type=jnp.float32)
    up = jnp.dot(x, up_ref[...], preferred_element_type=jnp.float32)
    for i, (which, row) in enumerate(places):
        here = slice(i * size, (i + 1) * size)
        weight = w_refs[which][pl.ds(row, 1), :]
        weight = jnp.sum(jnp.where(eye, weight, 0.0), axis=1, keepdims=True)
        hidden = gate[here] / (1.0 + jnp.exp(-gate[here])) * up[here] * weight
        out_ref[:, here] = hidden.T.astype(jnp.bfloat16)


def hidden_rows(blocks, weights, places, gate_w, up_w):
    depth, units = gate_w.shape
    rows = sum(x.size for x in blocks) // depth
    return pl.pallas_call(
        functools.partial(hidden_kernel, places, len(weights)),
        in_specs=[WHOLE] * (len(weights) + len(blocks) + 2),
        out_specs=WHOLE,
        out_shape=jax.ShapeDtypeStruct((units, rows), jnp.bfloat16),
        compiler_params=PARAMS,
        cost_estimate=pl.CostEstimate(
            flops=4 * rows * depth * units,
            bytes_accessed=2 * (rows * depth + 2 * depth * units + rows * units),
            transcendentals=rows * units,
        ),
        name="hidden_rows",
    )(*weights, *blocks, gate_w, up_w)


def base_kernel(keep, mom_ref, sel_ref, out_ref):
    per = COLS // TILE
    wide = sel_ref.shape[0]

    @pl.loop(0, mom_ref.shape[1] // COLS)
    def _(step):
        far = pl.ds(pl.multiple_of(step * COLS, COLS), COLS)
        tiles = [step * per + b for b in range(per)]
        for a in range(wide):
            high, low = split(DECAY * mom_ref[a * TILE : (a + 1) * TILE, far])
            both = jnp.concatenate([sel_ref[a, t] for t in tiles], axis=0)
            upper = jnp.concatenate([sel_ref[a, t, pl.ds(0, keep)] for t in tiles], axis=0)
            first = jnp.dot(both, high, preferred_element_type=jnp.float32)
            second = jnp.dot(upper, low, preferred_element_type=jnp.float32)
            for b in range(per):
                lanes = slice(b * TILE, (b + 1) * TILE)
                at = 2 * keep * b
                rows = first[at : at + keep, lanes] + first[at + keep : at + 2 * keep, lanes]
                rows = rows + second[keep * b : keep * (b + 1), lanes]
                out_ref[tiles[b], pl.ds(a * keep, keep), :] = rows


def base_rows(momentum, sel):
    wide, tiles, keep = sel.shape[0], sel.shape[1], sel.shape[2] // 2
    return pl.pallas_call(
        functools.partial(base_kernel, keep),
        in_specs=[WHOLE] * 2,
        out_specs=WHOLE,
        out_shape=jax.ShapeDtypeStruct((tiles, wide * keep, TILE), jnp.float32),
        compiler_params=PARAMS,
        cost_estimate=pl.CostEstimate(
            flops=100 * momentum.size, bytes_accessed=5 * momentum.size, transcendentals=0
        ),
        name="base_rows",
    )(momentum, sel)


def project_kernel(keep, *refs):
    h_refs, (sel_ref, out_ref) = refs[:-2], refs[-2:]
    wide, tiles = sel_ref.shape[:2]
    per = 4

    @pl.loop(0, tiles // per)
    def _(step):
        for a in range(wide):
            table = jnp.concatenate([sel_ref[a, step * per + b] for b in range(per)], axis=0)
            row = 0
            for h_ref in h_refs:
                here = pl.ds(row, h_ref.shape[1])
                row += h_ref.shape[1]
                units = h_ref[a * TILE : (a + 1) * TILE, :]
                both = jnp.dot(table, units, preferred_element_type=jnp.float32)
                for b in range(per):
                    at = 2 * keep * b
                    high, low = split(both[at : at + keep] + both[at + keep : at + 2 * keep])
                    out_ref[step * per + b, pl.ds(a * keep, keep), here] = high
                    out_ref[step * per + b, pl.ds((wide + a) * keep, keep), here] = low


def project_rows(hiddens, sel):
    wide, tiles, keep = sel.shape[0], sel.shape[1], sel.shape[2] // 2
    rows = sum(h.shape[1] for h in hiddens)
    return pl.pallas_call(
        functools.partial(project_kernel, keep),
        in_specs=[WHOLE] * (len(hiddens) + 1),
        out_specs=WHOLE,
        out_shape=jax.ShapeDtypeStruct((tiles, 2 * wide * keep, rows), jnp.bfloat16),
        compiler_params=PARAMS,
        cost_estimate=pl.CostEstimate(
            flops=4 * tiles * wide * keep * TILE * rows,
            bytes_accessed=4 * tiles * wide * keep * rows,
            transcendentals=0,
        ),
        name="project_rows",
    )(*hiddens, sel)


def gradient_rows(own_ref, g_refs, places, far, local):
    rows = [own_ref[i, :, far] for i in range(own_ref.shape[0])]
    for which, row in places:
        ref = g_refs[which]
        rows.append(ref[row, :, local] if len(ref.shape) == 3 else ref[:, local])
    return jnp.concatenate(rows, axis=0)


def sent_kernel(start, places, proj_ref, base_ref, own_ref, *refs):
    g_refs, out_ref = refs[:-1], refs[-1]
    half = out_ref.shape[1]
    for t in range(out_ref.shape[0]):
        lanes = slice(t * TILE, (t + 1) * TILE)
        far = slice(start + t * TILE, start + (t + 1) * TILE)
        grads = gradient_rows(own_ref, g_refs, places, far, lanes)
        tile = start // TILE + t
        both = jnp.dot(proj_ref[tile], grads, preferred_element_type=jnp.float32)
        out_ref[t] = both[:half] + both[half:] + base_ref[tile]


def sent_rows(start, size, project, base, own, grads, places):
    return pl.pallas_call(
        functools.partial(sent_kernel, start, places),
        in_specs=[WHOLE] * (3 + len(grads)),
        out_specs=WHOLE,
        out_shape=jax.ShapeDtypeStruct((size // TILE,) + base.shape[1:], jnp.float32),
        compiler_params=PARAMS,
        cost_estimate=pl.CostEstimate(
            flops=2 * project.shape[1] * project.shape[2] * size,
            bytes_accessed=2 * project.shape[2] * size,
            transcendentals=0,
        ),
        name="sent_rows",
    )(project, base, own, *grads)


def moment_kernel(start, h_count, places, keep, *refs):
    h_refs, own_ref = refs[:h_count], refs[h_count]
    g_refs = refs[h_count + 1 : h_count + 1 + len({which for which, _ in places})]
    mom_ref, sent_ref, selt_ref = refs[h_count + 1 + len(g_refs) :][:3]
    new_ref = refs[-1]
    step = pl.program_id(0)
    local = pl.ds(pl.multiple_of(step * COLS, COLS), COLS)
    far = pl.ds(pl.multiple_of(step * COLS + start, COLS), COLS)
    hidden = jnp.concatenate([r[...] for r in h_refs], axis=1)
    grads = gradient_rows(own_ref, g_refs, places, far, local)
    moment = DECAY * mom_ref[:, far] + jnp.dot(hidden, grads, preferred_element_type=jnp.float32)
    per = COLS // TILE
    for b in range(per):
        lanes = slice(b * TILE, (b + 1) * TILE)
        t = step * per + b
        for a in range(selt_ref.shape[0]):
            high, low = split(sent_ref[t, pl.ds(a * keep, keep), :])
            stack = jnp.concatenate([high, high, low], axis=0)
            removed = jnp.dot(selt_ref[a, start // TILE + t], stack, preferred_element_type=jnp.float32)
            rows = slice(a * TILE, (a + 1) * TILE)
            new_ref[rows, lanes] = moment[rows, lanes] - removed


def moment_columns(start, size, hiddens, own, grads, places, momentum, sent, selt, buffer):
    units, width = momentum.shape
    keep = selt.shape[3] // 3
    args = [*hiddens, own, *grads, momentum, sent, selt]
    specs = [WHOLE] * len(args)
    alias = {}
    if buffer is not None:
        specs.append(pl.BlockSpec(memory_space=pl.ANY))
        alias = {len(args): 0}
        args.append(buffer)
    rows = sum(h.shape[1] for h in hiddens)
    return pl.pallas_call(
        functools.partial(moment_kernel, start, len(hiddens), places, keep),
        grid=(size // COLS,),
        in_specs=specs,
        out_specs=pl.BlockSpec((units, COLS), lambda j: (0, j + start // COLS)),
        out_shape=jax.ShapeDtypeStruct((units, width), jnp.float32),
        input_output_aliases=alias,
        compiler_params=PARAMS,
        cost_estimate=pl.CostEstimate(
            flops=2 * rows * units * size,
            bytes_accessed=size * (8 * units + 2 * rows) + 2 * units * rows,
            transcendentals=0,
        ),
        name="moment_columns",
    )(*args)


def update_kernel(start, scale, mine_ref, theirs_ref, selt_ref, *refs):
    out_ref = refs[-1]
    step = pl.program_id(0)
    per = COLS // TILE
    keep = selt_ref.shape[3] // 3
    for b in range(per):
        t = step * per + b
        total = (mine_ref[t].astype(jnp.float32) + theirs_ref[t].astype(jnp.float32)) * scale
        for a in range(selt_ref.shape[0]):
            high, low = split(total[a * keep : (a + 1) * keep])
            stack = jnp.concatenate([high, high, low], axis=0)
            block = jnp.dot(selt_ref[a, start // TILE + t], stack, preferred_element_type=jnp.float32)
            out_ref[a * TILE : (a + 1) * TILE, b * TILE : (b + 1) * TILE] = block.astype(jnp.bfloat16)


def update_columns(start, mine, theirs, selt, scale, shape, buffer):
    size = mine.shape[0] * TILE
    args, specs, alias = [mine, theirs, selt], [WHOLE] * 3, {}
    if buffer is not None:
        specs.append(pl.BlockSpec(memory_space=pl.ANY))
        alias = {len(args): 0}
        args.append(buffer)
    return pl.pallas_call(
        functools.partial(update_kernel, start, scale),
        grid=(size // COLS,),
        in_specs=specs,
        out_specs=pl.BlockSpec((shape[0], COLS), lambda j: (0, j + start // COLS)),
        out_shape=jax.ShapeDtypeStruct(shape, jnp.bfloat16),
        input_output_aliases=alias,
        compiler_params=PARAMS,
        cost_estimate=pl.CostEstimate(
            flops=2 * 48 * shape[0] * size, bytes_accessed=3 * shape[0] * size, transcendentals=0
        ),
        name="update_columns",
    )(*args)


def layer(tokens, cotangent, combine, routing, gate_proj, up_proj, momentum, freq_rows):
    experts, replicas = lax.axis_size("expert"), lax.axis_size("outer")
    me = lax.axis_index("expert")
    gate_w, up_w, moment = gate_proj[0], up_proj[0], momentum[0, 0]
    passes, _, _ = tokens.shape
    square = experts == 4 and passes == 2

    def swap(array, mask):
        return lax.ppermute(array, "expert", [(e, e ^ mask) for e in range(experts)])

    named = routing[:, None, :, :] == jnp.arange(experts, dtype=jnp.int32)[None, :, None, None]
    weight = jnp.sum(jnp.where(named, combine[:, None, :, :], 0.0), axis=3)
    weight_for = lambda e: lax.dynamic_index_in_dim(weight, e, axis=1, keepdims=False)
    own_weight = weight_for(me)
    table = jnp.asarray(cosine_parts())
    slices, start = [], 0
    for size in CHUNKS:
        slices.append(cotangent[:, :, start : start + size])
        start += size

    hiddens = [hidden_rows([tokens], [own_weight], [(0, p) for p in range(passes)], gate_w, up_w)]
    sel, selt = chosen_rows(freq_rows[0], table)
    grads, places = [], []
    if square:
        x, y = swap(tokens, 1), swap(tokens, 2)
        weights = [swap(weight_for(me ^ m), m) for m in (1, 2, 3)]
        d0, d1 = swap(x[0], 2), swap(y[1], 1)
        hiddens.append(
            hidden_rows([x, y], weights[:2], [(0, 0), (0, 1), (1, 0), (1, 1)], gate_w, up_w)
        )
        hiddens.append(hidden_rows([d0, d1], weights[2:], [(0, 0), (0, 1)], gate_w, up_w))
        places = [(0, 0), (0, 1), (1, 0), (1, 1), (2, 0), (3, 0)]
        for piece in slices:
            x, y = swap(piece, 1), swap(piece, 2)
            grads.append([x, y, swap(x[0], 2), swap(y[1], 1)])
    else:
        for m in range(1, experts):
            scale = swap(weight_for(me ^ m), m)
            hiddens.append(
                hidden_rows([swap(tokens, m)], [scale], [(0, p) for p in range(passes)], gate_w, up_w)
            )
            places += [(m - 1, p) for p in range(passes)]
        grads = [[swap(piece, m) for m in range(1, experts)] for piece in slices]

    base = base_rows(moment, sel)
    project = project_rows(hiddens, sel)
    start, buffer, out = 0, None, None
    for size, pieces in zip(CHUNKS, grads):
        sent = sent_rows(start, size, project, base, cotangent, pieces, places)
        buffer = moment_columns(
            start, size, hiddens, cotangent, pieces, places, moment, sent, selt, buffer
        )
        mask = 1
        while True:
            theirs = lax.ppermute(sent, "outer", [(o, o ^ mask) for o in range(replicas)])
            mask *= 2
            if mask >= replicas:
                break
            sent = (sent.astype(jnp.float32) + theirs.astype(jnp.float32)).astype(jnp.bfloat16)
        out = update_columns(start, sent, theirs, selt, 1.0 / replicas, moment.shape, out)
        start += size
    return buffer[None, None], out[None]


def solution(mesh):
    placed = (
        P(None, ("outer", "expert"), None),
        P(None, ("outer", "expert"), None),
        P(None, ("outer", "expert"), None),
        P(None, ("outer", "expert"), None),
        P("expert", None, None),
        P("expert", None, None),
        P("outer", "expert", None, None),
        P("expert", None, None, None),
    )
    return jax.shard_map(
        layer,
        mesh=mesh,
        in_specs=placed,
        out_specs=(P("outer", "expert", None, None), P("expert", None, None)),
        check_vma=False,
    )
```
